32 devices in a mesh: groups: 2 (over x), events: 16 (over z, y, core).
Axes of the slice: x: 2, y: 2, z: 4, core: 2. Of those that a mesh axis runs over, the one named last changes fastest.
Arguments:
- waveforms: bfloat16 [64, 128, 1024], P(('groups', 'events')), parts along dimension 0, may hold values from -8 to 8
- matching: int32 [2, 32], P(None, 'groups'), parts along dimension 1, may hold values from 0 to 15, as said below
- available: int32 [64, 128, 2, 2], P(('groups', 'events')), parts along dimension 0, may hold values 0 or 1
Outputs:
- aligned_stack: bfloat16 [64, 128, 1024], P(('groups', 'events')), parts along dimension 0
- pair_scores: float32 [2, 64, 2, 128], P(None, ('groups', 'events')), parts along dimension 1
The draws below stay inside these ranges and needn't reach their ends.
There are 2 independent parts, one for each index of `groups`. The reference program is written for one: setup_inputs(seed, part) draws one part's arguments, and reference() takes and returns one part's arrays. A program takes and returns all parts, laid end to end along the dimension named above; each array names one. Nothing has to cross between parts.
Inputs may be any that keep to these rules, and one draw needn't show every extreme that they name: `matching`: in each round a block's partner is another block, and the partner of its partner is the block itself.
All inputs are finite; a program needn't handle non-finite values. No bound on the sum of `available` on one device may be relied on, other than what follows from the above.
Results may differ from the reference program's by a relative error of at most 0.018.
Values may be sent and summed in bfloat16 or wider, within the bound.
No kernel may reach another device: no remote copies, remote signals or barrier semaphores. Data moves between devices by JAX's collectives and lax.ppermute only.
A program may use at most 128 MiB of HBM per device.

```python
import math
import jax
import jax.numpy as jnp
from jax import lax

EB = 2
STATIONS = 128
SAMPLES = 1024
LAGS = 128
ROUNDS = 2
MLEN = 1152
NBLK = 16
NEV = 32


def draw_waveforms(key, part):
    keys = jax.random.split(jax.random.fold_in(key, 7), 1)
    noise = jax.random.normal(keys[0], (NEV, STATIONS, SAMPLES), jnp.float32)
    wave = noise
    return jnp.clip(wave, -8.0, 8.0).astype(jnp.bfloat16)


def draw_matching(key, part):
    rounds_list = []
    for which in range(ROUNDS):
        order = jax.random.permutation(jax.random.fold_in(key, which + 11), NBLK).astype(jnp.int32)
        first = order[0::2]
        second = order[1::2]
        partner = jnp.zeros((NBLK,), jnp.int32).at[first].set(second).at[second].set(first)
        rounds_list.append(partner)
    return jnp.stack(rounds_list).astype(jnp.int32)


def set_ends(entries, stream_key, low, largest):
    longest = entries.shape.index(max(entries.shape))
    spots = []
    for shift in (0, 1):
        where = [jax.random.randint(jax.random.fold_in(stream_key, axis), (), 0, length) for axis, length in enumerate(entries.shape)]
        where[longest] = (where[longest] + shift) % entries.shape[longest]
        spots.append(tuple(where))
    return entries.at[spots[0]].set(low).at[spots[1]].set(largest)


def setup_inputs(seed: int = 0, part: int = 0) -> dict:
    arg_keys = jax.random.split(jax.random.key(seed), 4)
    part_keys = jax.random.split(jax.random.fold_in(arg_keys[3], part), 4)
    return {
        "waveforms": draw_waveforms(jax.random.fold_in(jax.random.fold_in(arg_keys[3], part), 71), part),
        "matching": draw_matching(jax.random.fold_in(jax.random.fold_in(arg_keys[3], part), 71), part),
        "available": set_ends((jax.random.randint(part_keys[2], (NEV, STATIONS, ROUNDS, EB), 0, 4) < 3).astype(jnp.int32), jax.random.fold_in(part_keys[2], 1), 0, 1),
    }


def make_tables():
    times = jnp.arange(SAMPLES, dtype=jnp.int32)
    freqs = jnp.arange(MLEN, dtype=jnp.int32)
    lagset = (jnp.arange(LAGS, dtype=jnp.int32) - LAGS // 2) % MLEN
    angle_t = (times[:, None] * freqs[None, :] % MLEN).astype(jnp.float32) * (2.0 * math.pi / MLEN)
    angle_l = (freqs[:, None] * lagset[None, :] % MLEN).astype(jnp.float32) * (2.0 * math.pi / MLEN)
    forward = jnp.concatenate([jnp.cos(angle_t), -jnp.sin(angle_t)], axis=1).astype(jnp.bfloat16)
    corr_tab = (jnp.concatenate([jnp.cos(angle_l), -jnp.sin(angle_l)], axis=0) / MLEN).astype(jnp.bfloat16)
    spread_tab = jnp.concatenate([jnp.cos(angle_l).T, jnp.sin(angle_l).T], axis=1).astype(jnp.bfloat16)
    back_tab = (jnp.concatenate([jnp.cos(angle_t).T, -jnp.sin(angle_t).T], axis=0) / MLEN).astype(jnp.bfloat16)
    return (forward, corr_tab, spread_tab, back_tab)

def cross_spectra(spec, partner):
    other = spec[partner].astype(jnp.float32)
    own = spec[None, :, None].astype(jnp.float32)
    real_a, imag_a = (own[..., :MLEN], own[..., MLEN:])
    real_b, imag_b = (other[..., :MLEN], other[..., MLEN:])
    return jnp.concatenate([real_a * real_b + imag_a * imag_b, real_a * imag_b - imag_a * real_b], axis=-1).astype(jnp.bfloat16)

def stack_of(spec, partner, spread, back_tab):
    other = spec[partner].astype(jnp.float32)
    real_y, imag_y = (other[..., :MLEN], other[..., MLEN:])
    real_v, imag_v = (spread[..., :MLEN], spread[..., MLEN:])
    real_z = lax.optimization_barrier(jnp.sum(real_v * real_y - imag_v * imag_y, axis=(0, 2)))
    imag_z = lax.optimization_barrier(jnp.sum(real_v * imag_y + imag_v * real_y, axis=(0, 2)))
    zspec = jnp.concatenate([real_z, imag_z], axis=-1).astype(jnp.bfloat16)
    flat = jnp.dot(zspec.reshape(-1, 2 * MLEN), back_tab, preferred_element_type=jnp.float32)
    return flat.reshape(zspec.shape[:-1] + (SAMPLES,)).astype(jnp.bfloat16)

def reference(waveforms, matching, available):
    forward, corr_tab, spread_tab, back_tab = make_tables()
    blocks_of = jnp.repeat(matching, EB, axis=1)
    partner = (blocks_of[:, :, None] * EB + jnp.arange(EB, dtype=jnp.int32)[None, None, :]).astype(jnp.int32)
    station_waves = jnp.moveaxis(waveforms, 1, 0)
    station_flags = jnp.moveaxis(available, 1, 0).astype(jnp.float32)

    def score_step(total, inputs):
        wave, flags = inputs
        spec = jnp.dot(wave, forward, preferred_element_type=jnp.float32).astype(jnp.bfloat16)
        cross = cross_spectra(spec, partner)
        corr = jnp.dot(cross.reshape(-1, 2 * MLEN), corr_tab, preferred_element_type=jnp.float32)
        corr = corr.reshape(ROUNDS, NEV, EB, LAGS)
        return (total + jnp.transpose(flags, (1, 0, 2))[..., None] * corr, spec)
    start = jnp.zeros((ROUNDS, NEV, EB, LAGS), jnp.float32)
    total, all_spec = lax.scan(score_step, start, (station_waves, station_flags))
    scores = total * (2.0 / math.sqrt(SAMPLES * STATIONS))
    weights = jax.nn.softmax(scores, axis=-1).astype(jnp.bfloat16)
    spread = jnp.dot(weights.reshape(-1, LAGS), spread_tab, preferred_element_type=jnp.float32)
    spread = spread.reshape(ROUNDS, NEV, EB, 2 * MLEN)

    def stack_step(carry, spec):
        return (carry, stack_of(spec, partner, spread, back_tab))
    stacks = lax.scan(stack_step, jnp.zeros((), jnp.float32), all_spec)[1]
    return (jnp.moveaxis(stacks, 0, 1), scores)
```

```python
import functools
import math

import jax
import jax.numpy as jnp
from jax import lax
from jax.experimental import pallas as pl
from jax.experimental.pallas import tpu as pltpu
from jax.sharding import PartitionSpec as P

LAGS = 128
HALF = LAGS // 2
NT = (((1,), (1,)), ((), ()))
VMEM = pl.BlockSpec(memory_space=pltpu.VMEM)
SMEM = pl.BlockSpec(memory_space=pltpu.SMEM)


def spread_kernel(chips, pos_ref, x_ref, *out_refs):
    rows = x_ref.shape[0] // chips
    for k in range(chips):
        at = pl.multiple_of((pos_ref[0] ^ k) * rows, rows)
        wave = x_ref[pl.ds(at, rows), :].astype(jnp.float32)
        out_refs[k][...] = pltpu.roll(wave, HALF, axis=1).astype(x_ref.dtype)


def pick_kernel(chips, rounds, slot_ref, same_ref, mine_ref, other_ref, *out_refs):
    rows = mine_ref.shape[1]
    for k in range(chips):
        for r in range(rounds):
            slot = slot_ref[k * rounds + r]
            same = same_ref[k * rounds + r]

            @pl.when(same == 1)
            def _():
                out_refs[k][r * rows : (r + 1) * rows, :] = mine_ref[slot]

            @pl.when(same == 0)
            def _():
                out_refs[k][r * rows : (r + 1) * rows, :] = other_ref[slot]


def turn_kernel(events, flag_ref, x_ref, out_ref):
    stations = x_ref.shape[0] // events
    blocks = x_ref.shape[1] // LAGS
    pairs = out_ref.shape[0]
    row = lax.broadcasted_iota(jnp.int32, (LAGS, LAGS), 0)
    col = lax.broadcasted_iota(jnp.int32, (LAGS, LAGS), 1)
    flip = jnp.where(row + col == LAGS - 1, 1.0, 0.0).astype(jnp.bfloat16)
    for e in range(events):
        for b in range(blocks):
            wave = x_ref[e * stations : (e + 1) * stations, b * LAGS : (b + 1) * LAGS]
            turned = lax.dot_general(flip, wave, NT, preferred_element_type=jnp.float32)
            for p in range(pairs):
                masked = turned * flag_ref[e * pairs + p : e * pairs + p + 1, :]
                out_ref[p, e * LAGS : (e + 1) * LAGS, b * stations : (b + 1) * stations] = (
                    masked.astype(jnp.bfloat16)
                )


def align_kernel(events, rounds, scale, pos_ref, turned_ref, *refs):
    got_refs = refs[:-5]
    stack_ref, score_ref, held, wide, tall = refs[-5:]
    chunks = len(got_refs)
    samples = stack_ref.shape[1]
    stations = stack_ref.shape[0] // events
    blocks = samples // LAGS
    rows = got_refs[0].shape[0] // rounds
    for k in range(chunks):
        at = pl.multiple_of((pos_ref[0] ^ k) * rows, rows)
        for r in range(rounds):
            held[r, pl.ds(at, rows), :] = got_refs[k][r * rows : (r + 1) * rows, :]

    lane = lax.broadcasted_iota(jnp.int32, (1, LAGS), 1)
    low = jnp.where(lane < HALF, 1.0, 0.0).astype(jnp.bfloat16)
    high = jnp.where(lane < HALF, 0.0, 1.0).astype(jnp.bfloat16)
    for r in range(rounds):
        for j in range(events):
            left = 2 * LAGS * (r * events + j)
            for b in range(blocks + 1):
                c = b % blocks
                wave = held[r, j * stations : (j + 1) * stations, c * LAGS : (c + 1) * LAGS]
                if b == 0:
                    wave = wave * high
                if b == blocks:
                    wave = wave * low
                if b < blocks:
                    wide[b * stations : (b + 1) * stations, left : left + LAGS] = wave
                if b > 0:
                    wide[(b - 1) * stations : b * stations, left + LAGS : left + 2 * LAGS] = wave

    for r in range(rounds):
        for j in range(events):
            p = r * events + j
            left = 2 * LAGS * p
            prod = jnp.dot(
                turned_ref[p], wide[:, left : left + 2 * LAGS], preferred_element_type=jnp.float32
            )
            for e in range(events):
                part = prod[e * LAGS : (e + 1) * LAGS]
                part = pltpu.roll(part, LAGS + 1, axis=1, stride=1, stride_axis=0)
                line = jnp.sum(part, axis=0, keepdims=True)[:, :LAGS] * scale
                score_ref[(r * events + e) * events + j, :] = line[0]

    scores = score_ref[...]
    grown = jnp.exp(scores - jnp.max(scores, axis=1, keepdims=True))
    weights = grown / jnp.sum(grown, axis=1, keepdims=True)
    weights = weights.astype(jnp.bfloat16).astype(jnp.float32)
    for r in range(rounds):
        for j in range(events):
            left = 2 * LAGS * (r * events + j)
            for e in range(events):
                q = (r * events + e) * events + j
                line = jnp.concatenate([weights[q : q + 1], jnp.zeros((1, LAGS), jnp.float32)], axis=1)
                band = jnp.broadcast_to(line, (LAGS, 2 * LAGS))
                band = pltpu.roll(band, 0, axis=1, stride=1, stride_axis=0)
                tall[e * LAGS : (e + 1) * LAGS, left : left + 2 * LAGS] = band.astype(jnp.bfloat16)

    sums = lax.dot_general(wide[...], tall[...], NT, preferred_element_type=jnp.float32)
    for e in range(events):
        for b in range(blocks):
            stack_ref[e * stations : (e + 1) * stations, b * LAGS : (b + 1) * LAGS] = sums[
                b * stations : (b + 1) * stations, e * LAGS : (e + 1) * LAGS
            ].astype(stack_ref.dtype)


def body(devices, waveforms, matching, available):
    events, stations, samples = waveforms.shape
    rounds = matching.shape[0]
    pairs = rounds * events
    kind = waveforms.dtype
    total = events * stations
    wave = waveforms.reshape(total, samples)
    me = lax.axis_index("events").astype(jnp.int32)
    chips = devices // 2
    chip, core = me // 2, me % 2

    flags = jnp.transpose(available, (0, 2, 3, 1)).reshape(events * pairs, stations)
    turned = pl.pallas_call(
        functools.partial(turn_kernel, events),
        out_shape=jax.ShapeDtypeStruct((pairs, events * LAGS, total // events * samples // LAGS), kind),
        in_specs=[VMEM] * 2,
        out_specs=VMEM,
        cost_estimate=pl.CostEstimate(
            flops=2 * total * samples * LAGS, bytes_accessed=12 * total * samples, transcendentals=0
        ),
        name="turn",
    )(flags.astype(jnp.float32), wave)

    if chips <= 8 and chips & (chips - 1) == 0 and total % (16 * chips) == 0:
        rows = total // chips
        sent = pl.pallas_call(
            functools.partial(spread_kernel, chips),
            out_shape=[jax.ShapeDtypeStruct((rows, samples), kind)] * chips,
            in_specs=[SMEM, VMEM],
            out_specs=[VMEM] * chips,
            name="spread",
        )(chip.reshape(1), wave)
        held = [sent[0]]
        for k in range(1, chips):
            route = [(i, i ^ (2 * k)) for i in range(devices)]
            held.append(lax.ppermute(sent[k], "events", route))
        mine = jnp.stack(held)
        other = lax.ppermute(mine, "events", [(i, i ^ 1) for i in range(devices)])
        goal = 2 * (chip ^ jnp.arange(chips, dtype=jnp.int32)) + core
        source = jnp.transpose(matching[:, goal]).reshape(-1)
        picked = pl.pallas_call(
            functools.partial(pick_kernel, chips, rounds),
            out_shape=[jax.ShapeDtypeStruct((rounds * rows, samples), kind)] * chips,
            in_specs=[SMEM, SMEM, VMEM, VMEM],
            out_specs=[VMEM] * chips,
            name="pick",
        )((source // 2) ^ chip, (source % 2 == core).astype(jnp.int32), mine, other)
        got = [picked[0]]
        for k in range(1, chips):
            route = [(i, i ^ (2 * k)) for i in range(devices)]
            got.append(lax.ppermute(picked[k], "events", route))
        spot = chip.reshape(1)
    else:
        delayed = jnp.roll(wave, HALF, axis=1).reshape(devices, total // devices, samples)
        held = lax.all_to_all(delayed, "events", split_axis=0, concat_axis=0, tiled=True)
        picked = jnp.stack([held[matching[r]] for r in range(rounds)], axis=1)
        got = lax.all_to_all(picked, "events", split_axis=0, concat_axis=0, tiled=True)
        got = [jnp.swapaxes(got, 0, 1).reshape(rounds * total, samples)]
        spot = jnp.zeros((1,), jnp.int32)

    blocks = samples // LAGS
    stack, scores = pl.pallas_call(
        functools.partial(align_kernel, events, rounds, 2.0 / math.sqrt(samples * stations)),
        out_shape=(
            jax.ShapeDtypeStruct((total, samples), kind),
            jax.ShapeDtypeStruct((rounds * events * events, LAGS), jnp.float32),
        ),
        in_specs=[SMEM] + [VMEM] * (1 + len(got)),
        out_specs=(VMEM, VMEM),
        scratch_shapes=[
            pltpu.VMEM((rounds, total, samples), kind),
            pltpu.VMEM((blocks * stations, 2 * LAGS * pairs), kind),
            pltpu.VMEM((events * LAGS, 2 * LAGS * pairs), kind),
        ],
        name="align",
    )(spot, turned, *got)
    return (
        stack.reshape(events, stations, samples),
        scores.reshape(rounds, events, events, LAGS),
    )


def solution(mesh):
    placed = (
        P(("groups", "events"), None, None),
        P(None, "groups"),
        P(("groups", "events"), None, None, None),
    )
    return jax.shard_map(
        functools.partial(body, mesh.shape["events"]),
        mesh=mesh,
        in_specs=placed,
        out_specs=(P(("groups", "events"), None, None), P(None, ("groups", "events"), None, None)),
        check_vma=False,
    )
```
